32 devices in a mesh: expert: 16 (over z, y, x), tensor: 2 (over core).
Axes of the slice: x: 2, y: 2, z: 4, core: 2. Of those that a mesh axis runs over, the one named last changes fastest.
Arguments:
- tokens: bfloat16 [2048, 2048], P('expert'), may hold values from -40 to 40
- expert_ids: int32 [2048, 2], P('expert'), may hold values from 0 to 7, as said below
- positions: int32 [2048, 2], P('expert'), may hold values from -1 to 63, as said below
- gates: bfloat16 [2048, 2], P('expert'), may hold values from 0.099609375 to 0.8984375
- languages: int32 [2048], P('expert'), may hold values from 0 to 201
- ln_gain: bfloat16 [202, 2048], replicated, may hold values from 0.099609375 to 1.8984375
- ln_bias: bfloat16 [202, 2048], replicated, may hold values from -1.796875 to 1.796875
- w_in: bfloat16 [16, 2048, 2048], P('expert', None, 'tensor'), may hold values from -0.125 to 0.125
- w_out: bfloat16 [16, 2048, 2048], P('expert', 'tensor'), may hold values from -0.09375 to 0.09375
- w_qkv: bfloat16 [2048, 6144], P('expert', 'tensor'), may hold values from -0.125 to 0.125
Outputs:
- residual_out: bfloat16 [2048, 2048], P('expert', 'tensor')
- projected: bfloat16 [2048, 6144], P('expert', 'tensor')
The draws below stay inside these ranges and needn't reach their ends.
Inputs may be any that keep to these rules, and one draw needn't show every extreme that they name: `expert_ids`: the two experts of a token differ. Some expert is chosen at least 64 times among the tokens of every owner. `positions`: A choice's position is the number of earlier choices of the same owner naming the same expert (tokens in order, a token's first choice before its second), or -1 when that number is 64 or more.
All inputs are finite; a program needn't handle non-finite values.
Results may differ from the reference program's by a relative error of at most 0.0059.
Values may be sent and summed in bfloat16 or wider, within the bound.
No kernel may reach another device: no remote copies, remote signals or barrier semaphores. Data moves between devices by JAX's collectives and lax.ppermute only.
A program may use at most 128 MiB of HBM per device.

```python
import math
import jax
import jax.numpy as jnp
from jax import lax

D = 2048
FF = 4096
LANGS = 202
TOK_DEV = 128
EXPERTS = 8
CAP = 64
TOKENS = 2048
N_EXPERT = 16


def route_tables(key):
    base = jax.random.fold_in(key, 101)
    keys = jax.random.split(base, 6)
    owners = TOKENS // TOK_DEV
    order = jax.random.permutation(keys[0], EXPERTS).astype(jnp.int32)
    first_draw = jax.random.randint(keys[1], (TOKENS,), 0, EXPERTS)
    other_draw = jax.random.randint(keys[2], (TOKENS,), 0, EXPERTS)
    first = jnp.minimum(first_draw, other_draw)
    second = (first + jax.random.randint(keys[3], (TOKENS,), 1, EXPERTS)) % EXPERTS
    chosen = jax.random.randint(keys[4], (), 0, EXPERTS)
    owner_keys = jax.random.split(keys[5], owners)
    ranks = jax.vmap(lambda subkey: jax.random.permutation(subkey, TOK_DEV))(owner_keys).reshape(TOKENS)
    forced = ranks < CAP
    second = jnp.where(forced & (second == chosen), (chosen + 1) % EXPERTS, second)
    first = jnp.where(forced, chosen, first)
    identity = order[jnp.stack([first, second], axis=1)].astype(jnp.int32)
    flat_ids = identity.reshape(owners, TOK_DEV * 2)
    onehot = (flat_ids[:, :, None] == jnp.arange(EXPERTS, dtype=jnp.int32)[None, None, :]).astype(jnp.int32)
    earlier = jnp.cumsum(onehot, axis=1) - onehot
    ranked = jnp.sum(earlier * onehot, axis=2).reshape(TOKENS, 2)
    placed = jnp.where(ranked < CAP, ranked, -1).astype(jnp.int32)
    return (identity, placed)


def draw_expert_ids(key, part):
    identity, placed = route_tables(key)
    return identity


def draw_positions(key, part):
    identity, placed = route_tables(key)
    return placed


def draw_tokens(key, part):
    keys = jax.random.split(jax.random.fold_in(key, 202), 3)
    row_scale = jnp.exp(jax.random.uniform(keys[0], (TOKENS, 1), minval=math.log(0.5), maxval=math.log(5.0)))
    ramp = jnp.arange(D, dtype=jnp.float32) / D
    col_scale = 0.6 * jnp.exp(math.log(3.0) * ramp)[None, :] * jnp.exp(jax.random.uniform(keys[1], (1, D), minval=math.log(0.7), maxval=math.log(1.4)))
    values = jax.random.normal(keys[2], (TOKENS, D))
    return jnp.clip(row_scale * col_scale * values, -40.0, 40.0).astype(jnp.bfloat16)


def place_ends(values, stream_key, least, high):
    extent = values.shape
    spot = [jax.random.randint(jax.random.fold_in(stream_key, axis), (), 0, extent[axis]) for axis in range(len(extent))]
    values = values.at[tuple(spot)].set(least)
    longest = extent.index(max(extent))
    spot[longest] = (spot[longest] + 1) % extent[longest]
    return values.at[tuple(spot)].set(high)


def shard_levels(stream_key, extent, cuts, low, high):
    loudness = 1.0
    for axis_at, blocks in cuts:
        heights = jax.random.uniform(jax.random.fold_in(jax.random.fold_in(stream_key, 6), axis_at), (blocks,), jnp.float32, low / len(cuts), high / len(cuts))
        loudness = loudness * jnp.repeat(jnp.exp(heights), extent[axis_at] // blocks).reshape((-1,) + (1,) * (len(extent) - 1 - axis_at))
    return loudness


def normal_values(rng, extent, width, reach, pieces=(), kind=jnp.bfloat16):
    gain = shard_levels(rng, extent, pieces, -0.22, 0.18) if pieces else 1.0
    values = jax.random.normal(rng, extent, jnp.float32) * width * gain
    return jnp.minimum(jnp.maximum(values, -reach), reach).astype(kind)


def setup_inputs(seed: int = 0) -> dict:
    splits = jax.random.split(jax.random.key(seed), 11)
    tokens = draw_tokens(jax.random.fold_in(splits[10], 71), 0)
    expert_ids = draw_expert_ids(jax.random.fold_in(splits[10], 71), 0)
    positions = draw_positions(jax.random.fold_in(splits[10], 71), 0)
    gates = jnp.clip(0.099609375 + 0.7988281 * jax.random.uniform(splits[3], (TOKENS, 2), jnp.float32) ** shard_levels(splits[3], (TOKENS, 2), ((0, 16),), -0.2, 0.2), 0.099609375, 0.8984375).astype(jnp.bfloat16)
    languages = place_ends(jax.random.randint(splits[4], (TOKENS,), 0, LANGS), jax.random.fold_in(splits[4], 1), 0, LANGS - 1).astype(jnp.int32)
    ln_gain = jnp.clip(1.0 + 0.18 * jax.random.normal(splits[5], (LANGS, D), jnp.float32), 0.099609375, 1.8984375).astype(jnp.bfloat16)
    ln_bias = normal_values(splits[6], (LANGS, D), 0.3, 1.796875)
    w_in = normal_values(splits[7], (N_EXPERT, D, FF // 2), D ** -0.5, 0.125, ((0, 16), (2, 2)))
    w_out = normal_values(splits[8], (N_EXPERT, FF // 2, D), FF ** -0.5, 0.09375, ((0, 16), (1, 2)))
    w_qkv = normal_values(splits[9], (D, 3 * D), D ** -0.5, 0.125, ((0, 16), (1, 2)))
    return {"tokens": tokens, "expert_ids": expert_ids, "positions": positions, "gates": gates, "languages": languages, "ln_gain": ln_gain, "ln_bias": ln_bias, "w_in": w_in, "w_out": w_out, "w_qkv": w_qkv}


def layer_norm(values, gain_rows, bias_rows):
    center = values - lax.optimization_barrier(jnp.mean(values, axis=-1, keepdims=True))
    spread = lax.optimization_barrier(jnp.mean(center * center, axis=-1, keepdims=True))
    return center * lax.rsqrt(spread + 1e-05) * gain_rows + bias_rows

def reference(tokens, expert_ids, positions, gates, languages, ln_gain, ln_bias, w_in, w_out, w_qkv):
    owner_row = (jnp.arange(TOKENS, dtype=jnp.int32) // TOK_DEV)[:, None]
    slot_count = N_EXPERT * CAP

    def per_expert(summed, expert):
        picked_mask = (expert_ids == expert) & (positions >= 0)
        target = jnp.where(picked_mask, owner_row * CAP + positions, slot_count).astype(jnp.int32)
        gathered = jnp.zeros((slot_count, D), jnp.bfloat16)
        gathered = gathered.at[target[:, 0]].set(tokens, mode='drop')
        gathered = gathered.at[target[:, 1]].set(tokens, mode='drop')
        first_w = jnp.concatenate([w_in[2 * expert], w_in[2 * expert + 1]], axis=1)
        second_w = jnp.concatenate([w_out[2 * expert], w_out[2 * expert + 1]], axis=0)
        hidden = jnp.maximum(jnp.dot(gathered, first_w, preferred_element_type=jnp.float32), 0.0).astype(jnp.bfloat16)
        outputs = jnp.dot(hidden, second_w, preferred_element_type=jnp.float32).astype(jnp.bfloat16)
        fetched = outputs[jnp.minimum(target, slot_count - 1)].astype(jnp.float32)
        weight = jnp.where(picked_mask, gates.astype(jnp.float32), jnp.zeros_like(gates, dtype=jnp.float32))
        return (summed + lax.optimization_barrier(jnp.sum(fetched * weight[:, :, None], axis=1)), None)
    combined, unused = lax.scan(per_expert, jnp.zeros((TOKENS, D), jnp.float32), jnp.arange(EXPERTS, dtype=jnp.int32))
    residual_out = (tokens.astype(jnp.float32) + combined).astype(jnp.bfloat16)
    gain_rows = ln_gain[languages].astype(jnp.float32)
    bias_rows = ln_bias[languages].astype(jnp.float32)
    normed = layer_norm(residual_out.astype(jnp.float32), gain_rows, bias_rows).astype(jnp.bfloat16)
    projected = jnp.dot(normed, w_qkv, preferred_element_type=jnp.float32).astype(jnp.bfloat16)
    return (residual_out, projected)
```

```python
import jax
import jax.numpy as jnp
from jax import lax
from jax.sharding import PartitionSpec as P


CHUNKS = ((0,), (8,), (12,), (4,))


def across(array):
    return lax.ppermute(array, "tensor", [(0, 1), (1, 0)])


def partner(array, mask):
    pairs = [(i, i ^ mask) for i in range(lax.axis_size("expert"))]
    return lax.ppermute(array, "expert", pairs)


def dot(a, b):
    return jnp.dot(a, b, preferred_element_type=jnp.float32)


def after(value, other):
    return lax.optimization_barrier((value, other))[0]


def ordered(pieces, index):
    bit = 1
    while bit < len(pieces):
        swap = (index & bit) != 0
        pieces = [jnp.where(swap, pieces[j ^ bit], pieces[j]) for j in range(len(pieces))]
        bit *= 2
    return pieces


def projection_weights(w_qkv, me, core):
    devices = lax.axis_size("expert")
    top = devices.bit_length() - 2
    _, columns = w_qkv.shape
    part = columns // 4
    first, third = me & 1, (me >> 2) & 1

    def columns_of(array, which):
        return lax.dynamic_slice_in_dim(array, which * (array.shape[-1] // 2), array.shape[-1] // 2, array.ndim - 1)

    away = partner(columns_of(w_qkv, 1 - first), 1)
    block = jnp.stack(ordered([columns_of(w_qkv, first), away], first))
    away = partner(columns_of(block, 1 - third), 4)
    block = jnp.stack(ordered([columns_of(block, third), away], third))
    halves = [block, partner(block, 1 << top)]
    bits = [2, 0]
    for bit in [1] + list(range(3, top)):
        for i in (0, 1):
            pair = [halves[i], partner(halves[i], 1 << bit)]
            halves[i] = jnp.stack(ordered(pair, (me >> bit) & 1))
        bits = [bit] + bits
    order = [bits.index(b) for b in range(top - 1, -1, -1)]
    for i in (0, 1):
        halves[i] = halves[i].transpose(*order, top, top + 1).reshape(-1, part)
    same = ((me >> top) & 1) == core
    return jnp.where(same, halves[0], halves[1]), jnp.where(same, halves[1], halves[0])


def on_device(
    tokens, expert_ids, positions, gates, languages, ln_gain, ln_bias, w_in, w_out, w_qkv
):
    tok, width = tokens.shape
    half = width // 2
    devices = lax.axis_size("expert")
    outer_bits = range(4, devices.bit_length() - 1)
    outer = devices // 16
    capacity = max(2, 4 * tok // (devices // 2))
    me = lax.axis_index("expert")
    core = lax.axis_index("tensor")

    def own_columns(array, which):
        return lax.dynamic_slice_in_dim(array, which * half, half, 1)

    slot_ids = jnp.where(positions >= 0, expert_ids * capacity + positions, -1)
    table = jnp.concatenate([slot_ids.astype(jnp.float32), gates.astype(jnp.float32)], axis=1).T

    own = own_columns(tokens, core)
    block = own[None]
    table = table[None]
    for bit in outer_bits:
        block = jnp.concatenate([block, partner(block, 1 << bit)])
        table = jnp.concatenate([table, partner(table, 1 << bit)])
    blocks = {0: block, 8: partner(block, 8), 4: partner(block, 4)}
    blocks[12] = partner(blocks[8], 4)
    places = {0: table, 8: partner(table, 8), 4: partner(table, 4)}
    places[12] = partner(places[8], 4)

    expert = me >> 1
    slots = jnp.concatenate(
        [e * capacity + lax.iota(jnp.int32, capacity) for e in (expert, expert ^ 1)]
    ).astype(jnp.float32)

    wi = [lax.dynamic_slice_in_dim(w_in[0], c * half, half, 0) for c in (core, 1 - core)]
    wo = [own_columns(w_out[0], c) for c in (core, 1 - core)]
    w_own, w_other = projection_weights(w_qkv, me, core)

    def dispatch(distances, ready):
        rows = []
        for d in distances:
            place = places[d] if ready is None else after(places[d], ready)
            matches = place[:, :2, None, :] == slots[None, None, :, None]
            placing = jnp.any(matches, axis=1).astype(jnp.bfloat16)
            rows.append(
                [
                    jnp.einsum(
                        "rst,rtd->rsd", part, blocks[d], preferred_element_type=jnp.float32
                    ).astype(jnp.bfloat16)
                    for part in (placing[:, :capacity], placing[:, capacity:])
                ]
            )
        kept, given = [jnp.concatenate(r).reshape(-1, half) for r in zip(*rows)]
        pair = jnp.concatenate([kept, partner(given, 2)])
        mine = jnp.concatenate([pair, partner(pair, 1)])
        return (mine, across(mine)), given

    def experts(mine, other):
        hidden = jnp.maximum(dot(mine, wi[0]) + dot(other, wi[1]), 0.0).astype(jnp.bfloat16)
        away = dot(hidden, wo[1]).astype(jnp.bfloat16)
        away = across(away)
        return dot(hidden, wo[0]) + away.astype(jnp.float32)

    def combine(distances, sums):
        count = sums.shape[0] // 4
        away = partner(sums[2 * count :].astype(jnp.bfloat16), 1)
        sums = (sums[: 2 * count] + away.astype(jnp.float32)).astype(jnp.bfloat16)
        far = partner(sums[count:], 2)
        results = {}
        near = sums[:count].reshape(len(distances), outer, capacity, half)
        far = far.reshape(len(distances), outer, capacity, half)
        for j, d in enumerate(distances):
            matches = places[d][:, :2, :, None] == slots[None, None, None, :]
            weights = jnp.sum(jnp.where(matches, places[d][:, 2:, :, None], 0.0), axis=1)
            results[d] = jnp.einsum(
                "rts,rsd->rtd",
                weights.astype(jnp.bfloat16),
                jnp.concatenate([near[j], far[j]], axis=1),
                preferred_element_type=jnp.float32,
            )
        return results

    parts, ready = {}, None
    for distances in CHUNKS:
        received, ready = dispatch(distances, ready)
        parts.update(combine(distances, experts(*received)))

    def moved(value, mask):
        return partner(value.astype(jnp.bfloat16), mask).astype(jnp.float32)

    total = parts[0] + moved(parts[4], 4)
    total += moved(parts[8], 8) + moved(parts[12], 12)
    for bit in reversed(outer_bits):
        count = total.shape[0] // 2
        total = total[:count] + moved(total[count:], 1 << bit)

    residual = (own.astype(jnp.float32) + total[0]).astype(jnp.bfloat16)

    values = residual.astype(jnp.float32)
    local_mean = jnp.mean(values, axis=1, keepdims=True)
    local = values - local_mean
    stats = jnp.concatenate([local_mean, jnp.sum(local * local, axis=1, keepdims=True)], axis=1)
    other_stats = across(stats)
    gap = local_mean - other_stats[:, :1]
    mean = local_mean - gap * 0.5
    spread = (stats[:, 1:] + other_stats[:, 1:] + gap * gap * (half * 0.5)) / width
    lang_hot = (languages[:, None] == lax.iota(jnp.int32, ln_gain.shape[0])[None, :]).astype(
        jnp.bfloat16
    )
    gain_rows = dot(lang_hot, own_columns(ln_gain, core))
    bias_rows = dot(lang_hot, own_columns(ln_bias, core))
    normed = ((values - mean) * lax.rsqrt(spread + 1e-05) * gain_rows + bias_rows).astype(
        jnp.bfloat16
    )

    def project(block):
        other = across(block)
        return (dot(block, w_own) + dot(other, w_other)).astype(jnp.bfloat16)

    quarter = (me & 1) * 2 | ((me >> 2) & 1)
    arrived = {mask: partner(normed, mask) for mask in (5, 1, 4)}
    pieces = {0: project(normed)}
    for mask, block in arrived.items():
        pieces[mask] = partner(project(block), mask)
    pieces = [pieces[mask] for mask in (0, 4, 1, 5)]
    projected = jnp.concatenate(ordered(pieces, quarter), axis=1)
    return (residual, projected)


def solution(mesh):
    in_specs = (
        P("expert", None),
        P("expert", None),
        P("expert", None),
        P("expert", None),
        P("expert"),
        P(),
        P(),
        P("expert", None, "tensor"),
        P("expert", "tensor", None),
        P("expert", "tensor"),
    )
    out_specs = (P("expert", "tensor"), P("expert", "tensor"))

    return jax.shard_map(
        on_device, mesh=mesh, in_specs=in_specs, out_specs=out_specs, check_vma=False
    )
```

```python
import jax
import jax.numpy as jnp
from jax import lax
from jax.sharding import PartitionSpec as P


CHUNKS = ((0,), (8,), (12,), (4,))


def across(array):
    return lax.ppermute(array, "tensor", [(0, 1), (1, 0)])


def partner(array, mask):
    pairs = [(i, i ^ mask) for i in range(lax.axis_size("expert"))]
    return lax.ppermute(array, "expert", pairs)


def dot(a, b):
    return jnp.dot(a, b, preferred_element_type=jnp.float32)


def after(value, other):
    return lax.optimization_barrier((value, other))[0]


def ordered(pieces, index):
    bit = 1
    while bit < len(pieces):
        swap = (index & bit) != 0
        pieces = [jnp.where(swap, pieces[j ^ bit], pieces[j]) for j in range(len(pieces))]
        bit *= 2
    return pieces


def projection_weights(w_qkv, me, core):
    devices = lax.axis_size("expert")
    top = devices.bit_length() - 2
    _, columns = w_qkv.shape
    part = columns // 4
    first, third = me & 1, (me >> 2) & 1

    def columns_of(array, which):
        return lax.dynamic_slice_in_dim(array, which * (array.shape[-1] // 2), array.shape[-1] // 2, array.ndim - 1)

    away = partner(columns_of(w_qkv, 1 - first), 1)
    block = jnp.stack(ordered([columns_of(w_qkv, first), away], first))
    away = partner(columns_of(block, 1 - third), 4)
    block = jnp.stack(ordered([columns_of(block, third), away], third))
    halves = [block, partner(block, 1 << top)]
    bits = [2, 0]
    for bit in [1] + list(range(3, top)):
        for i in (0, 1):
            pair = [halves[i], partner(halves[i], 1 << bit)]
            halves[i] = jnp.stack(ordered(pair, (me >> bit) & 1))
        bits = [bit] + bits
    order = [bits.index(b) for b in range(top - 1, -1, -1)]
    for i in (0, 1):
        halves[i] = halves[i].transpose(*order, top, top + 1).reshape(-1, part)
    same = ((me >> top) & 1) == core
    return jnp.where(same, halves[0], halves[1]), jnp.where(same, halves[1], halves[0])


def on_device(
    tokens, expert_ids, positions, gates, languages, ln_gain, ln_bias, w_in, w_out, w_qkv
):
    tok, width = tokens.shape
    half = width // 2
    devices = lax.axis_size("expert")
    outer_bits = range(4, devices.bit_length() - 1)
    outer = devices // 16
    capacity = max(2, 4 * tok // (devices // 2))
    me = lax.axis_index("expert")
    core = lax.axis_index("tensor")

    def own_columns(array, which):
        return lax.dynamic_slice_in_dim(array, which * half, half, 1)

    slot_ids = jnp.where(positions >= 0, expert_ids * capacity + positions, -1)
    table = jnp.concatenate([slot_ids.astype(jnp.float32), gates.astype(jnp.float32)], axis=1).T

    own = own_columns(tokens, core)
    block = own[None]
    table = table[None]
    for bit in outer_bits:
        block = jnp.concatenate([block, partner(block, 1 << bit)])
        table = jnp.concatenate([table, partner(table, 1 << bit)])
    blocks = {0: block, 8: partner(block, 8), 4: partner(block, 4)}
    blocks[12] = partner(blocks[8], 4)
    places = {0: table, 8: partner(table, 8), 4: partner(table, 4)}
    places[12] = partner(places[8], 4)

    expert = me >> 1
    slots = jnp.concatenate(
        [e * capacity + lax.iota(jnp.int32, capacity) for e in (expert, expert ^ 1)]
    ).astype(jnp.float32)

    wi = [lax.dynamic_slice_in_dim(w_in[0], c * half, half, 0) for c in (core, 1 - core)]
    wo = [own_columns(w_out[0], c) for c in (core, 1 - core)]
    w_own, w_other = projection_weights(w_qkv, me, core)

    def dispatch(distances, ready):
        rows = []
        for d in distances:
            place = places[d] if ready is None else after(places[d], ready)
            matches = place[:, :2, None, :] == slots[None, None, :, None]
            placing = jnp.any(matches, axis=1).astype(jnp.bfloat16)
            rows.append(
                [
                    jnp.einsum(
                        "rst,rtd->rsd", part, blocks[d], preferred_element_type=jnp.float32
                    ).astype(jnp.bfloat16)
                    for part in (placing[:, :capacity], placing[:, capacity:])
                ]
            )
        kept, given = [jnp.concatenate(r).reshape(-1, half) for r in zip(*rows)]
        pair = jnp.concatenate([kept, partner(given, 2)])
        mine = jnp.concatenate([pair, partner(pair, 1)])
        return (mine, across(mine)), given

    def experts(mine, other):
        hidden = jnp.maximum(dot(mine, wi[0]) + dot(other, wi[1]), 0.0).astype(jnp.bfloat16)
        away = dot(hidden, wo[1]).astype(jnp.bfloat16)
        away = across(away)
        return dot(hidden, wo[0]) + away.astype(jnp.float32)

    def combine(distances, sums):
        count = sums.shape[0] // 4
        away = partner(sums[2 * count :].astype(jnp.bfloat16), 1)
        sums = (sums[: 2 * count] + away.astype(jnp.float32)).astype(jnp.bfloat16)
        far = partner(sums[count:], 2)
        results = {}
        near = sums[:count].reshape(len(distances), outer, capacity, half)
        far = far.reshape(len(distances), outer, capacity, half)
        for j, d in enumerate(distances):
            matches = places[d][:, :2, :, None] == slots[None, None, None, :]
            weights = jnp.sum(jnp.where(matches, places[d][:, 2:, :, None], 0.0), axis=1)
            results[d] = jnp.einsum(
                "rts,rsd->rtd",
                weights.astype(jnp.bfloat16),
                jnp.concatenate([near[j], far[j]], axis=1),
                preferred_element_type=jnp.float32,
            )
        return results

    received, ready = {}, None
    for i in (0, 1, 3, 2):
        received[i], ready = dispatch(CHUNKS[i], ready)
    parts = {}
    for i, distances in enumerate(CHUNKS):
        parts.update(combine(distances, experts(*received[i])))

    def moved(value, mask):
        return partner(value.astype(jnp.bfloat16), mask).astype(jnp.float32)

    total = parts[0] + moved(parts[4], 4)
    total += moved(parts[8], 8) + moved(parts[12], 12)
    for bit in reversed(outer_bits):
        count = total.shape[0] // 2
        total = total[:count] + moved(total[count:], 1 << bit)

    residual = (own.astype(jnp.float32) + total[0]).astype(jnp.bfloat16)

    values = residual.astype(jnp.float32)
    local_mean = jnp.mean(values, axis=1, keepdims=True)
    local = values - local_mean
    stats = jnp.concatenate([local_mean, jnp.sum(local * local, axis=1, keepdims=True)], axis=1)
    other_stats = across(stats)
    gap = local_mean - other_stats[:, :1]
    mean = local_mean - gap * 0.5
    spread = (stats[:, 1:] + other_stats[:, 1:] + gap * gap * (half * 0.5)) / width
    lang_hot = (languages[:, None] == lax.iota(jnp.int32, ln_gain.shape[0])[None, :]).astype(
        jnp.bfloat16
    )
    gain_rows = dot(lang_hot, own_columns(ln_gain, core))
    bias_rows = dot(lang_hot, own_columns(ln_bias, core))
    normed = ((values - mean) * lax.rsqrt(spread + 1e-05) * gain_rows + bias_rows).astype(
        jnp.bfloat16
    )

    def project(block):
        other = across(block)
        return (dot(block, w_own) + dot(other, w_other)).astype(jnp.bfloat16)

    quarter = (me & 1) * 2 | ((me >> 2) & 1)
    arrived = {mask: partner(normed, mask) for mask in (5, 1, 4)}
    pieces = {0: project(normed)}
    for mask, block in arrived.items():
        pieces[mask] = partner(project(block), mask)
    pieces = [pieces[mask] for mask in (0, 4, 1, 5)]
    projected = jnp.concatenate(ordered(pieces, quarter), axis=1)
    return (residual, projected)


def solution(mesh):
    in_specs = (
        P("expert", None),
        P("expert", None),
        P("expert", None),
        P("expert", None),
        P("expert"),
        P(),
        P(),
        P("expert", None, "tensor"),
        P("expert", "tensor", None),
        P("expert", "tensor"),
    )
    out_specs = (P("expert", "tensor"), P("expert", "tensor"))

    return jax.shard_map(
        on_device, mesh=mesh, in_specs=in_specs, out_specs=out_specs, check_vma=False
    )
```
